256 devices in a mesh: dp: 4 (over y), expert: 64 (over z, x, core).
Axes of the slice: x: 4, y: 4, z: 8, core: 2. Of those that a mesh axis runs over, the one named last changes fastest.
Arguments:
- tokens: bfloat16 [8192, 2048], P(('dp', 'expert')), may hold values from -6 to 6
- routes: int32 [8192, 8], P(('dp', 'expert')), may hold values from 0 to 63, all different within a row; in each aligned block of 32 rows (0 to 31, 32 to 63, ...) at most 6 rows name the same one
- gates: float32 [8192, 8], P(('dp', 'expert')), may hold values from 0.1 to 0.6
- w_gate: bfloat16 [64, 2048, 768], P('expert'), may hold values from -0.125 to 0.125
- w_up: bfloat16 [64, 2048, 768], P('expert'), may hold values from -0.125 to 0.125
- w_down: bfloat16 [64, 768, 2048], P('expert'), may hold values from -0.21875 to 0.21875
- swap_flags: int32 [64], replicated, may hold values from 0 to 1, as said below
- d_out: bfloat16 [8192, 2048], P(('dp', 'expert')), may hold values from -6 to 6
Outputs:
- mixture: bfloat16 [8192, 2048], P(('dp', 'expert'))
- d_tokens: bfloat16 [8192, 2048], P(('dp', 'expert'))
- d_gates: float32 [8192, 8], P(('dp', 'expert'))
- g_gate: bfloat16 [64, 2048, 768], P('expert', 'dp')
- g_up: bfloat16 [64, 2048, 768], P('expert', 'dp')
- g_down: bfloat16 [64, 768, 2048], P('expert', None, 'dp')
The draws below stay inside these ranges and needn't reach their ends.
Inputs may be any that keep to these rules, and one draw needn't show every extreme that they name: `routes`: among the 32 rows of one device no expert is named more than 6 times, and in every draw some device names some expert exactly 6 times. swap_flags[i] equals swap_flags[i + 32]; swap_flags[0] and swap_flags[31] are 1.
All inputs are finite; a program needn't handle non-finite values.
Results may differ from the reference program's by a relative error of at most 0.0095.
Values may be sent and summed in bfloat16 or wider, within the bound.
No kernel may reach another device: no remote copies, remote signals or barrier semaphores. Data moves between devices by JAX's collectives and lax.ppermute only.
A program may use at most 128 MiB of HBM per device.

```python
import math
import jax
import jax.numpy as jnp
import numpy as np
from jax import lax

D = 2048
FF = 768
TOPK = 8
TOK_DEV = 32
EXPERTS = 64
CAP = 6
TOKENS = 8192
N_DP = 4
N_EXPERT = 64


def draw_swap_flags(key, part):
    pair_bits = jax.random.randint(key, (EXPERTS // 2,), 0, 2).astype(jnp.int32)
    pair_bits = pair_bits.at[0].set(1).at[EXPERTS // 2 - 1].set(1)
    return jnp.concatenate([pair_bits, pair_bits])


def level_of(own_key, extent, split, low, top_value):
    def one(dim, shards_of):
        heights = jax.random.uniform(jax.random.fold_in(jax.random.fold_in(own_key, 6), dim), (shards_of,), jnp.float32, low / len(split), top_value / len(split))
        return jnp.repeat(jnp.exp(heights), extent[dim] // shards_of).reshape((-1,) + (1,) * (len(extent) - dim - 1))

    level = one(*split[0])
    for cut in split[1:]:
        level = level * one(*cut)
    return level


def deal_out(rng, own, number, rows, amount, top, most, skew):
    ranking = jax.random.permutation(rng, amount)
    crowded, common = load_shares(amount, rows * top, most, skew, True), load_shares(amount, rows * top, most, skew, False)
    places = jnp.arange(amount)

    def named(tallies, rotation):
        used = int((tallies > 0).sum())
        fixed = max(1, used // 4)
        passed = fixed + (places - fixed + rotation * (used - fixed)) % max(1, amount - fixed)
        return jnp.zeros((amount,), jnp.int32).at[ranking[jnp.where(places < fixed, places, passed)]].set(jnp.asarray(tallies, jnp.int32))

    tallies = jnp.where(number % 4 == 0, named(crowded, number // 4), named(common, number - number // 4 - 1))
    mixed = jax.random.permutation(jax.random.fold_in(own, 3), amount)
    giver, taker = mixed[0:amount // 2 * 2:2], mixed[1:amount // 2 * 2:2]
    room = jnp.minimum(tallies[giver] - 1, most - tallies[taker]) // 2
    room = jnp.where((giver == ranking[0]) | (taker == ranking[0]) | (tallies[taker] == 0), 0, jnp.maximum(room, 0))
    passed = jax.random.randint(jax.random.fold_in(own, 4), (amount // 2,), 0, 1 << 20) % (room + 1)
    tallies = tallies.at[giver].add(-passed).at[taker].add(passed)
    labels = jnp.searchsorted(jnp.cumsum(tallies), jnp.arange(rows * top), side="right").astype(jnp.int32)
    listing = labels.reshape(top, rows).T
    listing = listing[jax.random.permutation(jax.random.fold_in(own, 1), rows)]
    rotation = jax.random.randint(jax.random.fold_in(own, 2), (rows, 1), 0, top)
    return jnp.take_along_axis(listing, (jnp.arange(top)[None, :] + rotation) % top, axis=1)


def load_shares(count, total, limit, slope, full):
    weights = [(1 << 20) // math.isqrt(standing ** slope) + 1 for standing in range(1, count + 1)]
    largest = limit if full else min(limit, max(-(-total // count), total * weights[0] // sum(weights)))
    least = 1 if total - largest >= count - 1 else 0
    counts, spare = [largest] + [least] * (count - 1), total - largest - least * (count - 1)
    while spare > 0:
        movable = [i for i in range(1, count) if counts[i] < largest] or [i for i in range(1, count) if counts[i] < limit]
        mass, left = sum([weights[i] for i in movable]), spare
        for i in movable:
            addition = min(limit - counts[i], max(1, left * weights[i] // mass), spare)
            counts[i] = counts[i] + addition
            spare = spare - addition
    return np.array(counts)


def normal_values(stream_key, dims, scale, bound, shards=(), kind=jnp.bfloat16):
    level = level_of(stream_key, dims, shards, -0.22, 0.18) if shards else 1.0
    values = jax.random.normal(stream_key, dims, jnp.float32) * scale * level
    return jnp.minimum(jnp.maximum(values, -bound), bound).astype(kind)


def setup_inputs(seed: int = 0) -> dict:
    arg_keys = jax.random.split(jax.random.key(seed), 9)
    tokens = normal_values(arg_keys[0], (TOKENS, D), 1.0, 6.0, ((0, 256),))
    routes_keys = jax.random.split(jax.random.fold_in(arg_keys[1], 1), TOKENS // TOK_DEV)
    routes_turns = jax.random.permutation(jax.random.fold_in(arg_keys[1], 3), TOKENS // TOK_DEV)
    routes = jax.vmap(lambda own, number: deal_out(jax.random.fold_in(arg_keys[1], 2), own, number, TOK_DEV, EXPERTS, TOPK, CAP, 2))(routes_keys, routes_turns).reshape((TOKENS, TOPK))
    gates = jnp.clip(0.1 + 0.5 * jax.random.uniform(arg_keys[2], (TOKENS, TOPK), jnp.float32) ** level_of(arg_keys[2], (TOKENS, TOPK), ((0, 256),), -0.2, 0.2), 0.1, 0.6)
    w_gate = normal_values(arg_keys[3], (EXPERTS, D, FF), D ** -0.5, 0.125, ((0, 64),))
    w_up = normal_values(arg_keys[4], (EXPERTS, D, FF), D ** -0.5, 0.125, ((0, 64),))
    w_down = normal_values(arg_keys[5], (EXPERTS, FF, D), FF ** -0.5, 0.21875, ((0, 64),))
    swap_flags = draw_swap_flags(jax.random.fold_in(arg_keys[8], 71), 0)
    d_out = normal_values(arg_keys[7], (TOKENS, D), 1.0, 6.0, ((0, 256),))
    return {"tokens": tokens, "routes": routes, "gates": gates, "w_gate": w_gate, "w_up": w_up, "w_down": w_down, "swap_flags": swap_flags, "d_out": d_out}


def expert_pass(inputs):
    w_gate_one, w_up_one, w_down_one, slot_token, slot_pair, slot_alive, token_table, expert_cot = inputs
    gate_f = w_gate_one.astype(jnp.float32)
    up_f = w_up_one.astype(jnp.float32)
    down_f = w_down_one.astype(jnp.float32)
    rows_in = token_table[slot_token].astype(jnp.float32) * slot_alive[:, None]
    cot_rows = expert_cot[slot_pair].astype(jnp.float32) * slot_alive[:, None]
    pre_gate = jnp.dot(rows_in, gate_f)
    pre_up = jnp.dot(rows_in, up_f)
    logistic = jax.nn.sigmoid(pre_gate)
    activated = pre_gate * logistic
    hidden = (activated * pre_up).astype(jnp.bfloat16)
    expert_out = jnp.dot(hidden.astype(jnp.float32), down_f).astype(jnp.bfloat16)
    d_hidden = jnp.dot(cot_rows, down_f.T)
    grad_gate_pre = (d_hidden * pre_up * logistic * (1.0 + pre_gate * (1.0 - logistic))).astype(jnp.bfloat16)
    grad_up_pre = (d_hidden * activated).astype(jnp.bfloat16)
    d_part = (jnp.dot(grad_gate_pre.astype(jnp.float32), gate_f.T) + jnp.dot(grad_up_pre.astype(jnp.float32), up_f.T)).astype(jnp.bfloat16)
    rows_grp = rows_in.reshape(N_DP, -1, D)
    gate_grp = grad_gate_pre.astype(jnp.float32).reshape(N_DP, -1, FF)
    up_grp = grad_up_pre.astype(jnp.float32).reshape(N_DP, -1, FF)
    hid_grp = hidden.astype(jnp.float32).reshape(N_DP, -1, FF)
    cot_grp = cot_rows.reshape(N_DP, -1, D)

    def reduce_rows(partial_value):
        rounded = lax.optimization_barrier(partial_value.astype(jnp.bfloat16))
        return jnp.sum(rounded.astype(jnp.float32), axis=0).astype(jnp.bfloat16)

    grad_gate = reduce_rows(jnp.einsum('rnd,rnf->rdf', rows_grp, gate_grp))
    grad_up = reduce_rows(jnp.einsum('rnd,rnf->rdf', rows_grp, up_grp))
    grad_down = reduce_rows(jnp.einsum('rnf,rnd->rfd', hid_grp, cot_grp))
    return expert_out, d_part, grad_gate, grad_up, grad_down


def reference(tokens, routes, gates, w_gate, w_up, w_down, swap_flags, d_out):
    devices = N_DP * N_EXPERT
    per_device = TOK_DEV * TOPK
    route_flat = routes.reshape(devices, per_device)
    onehot = (route_flat[:, :, None] == jnp.arange(EXPERTS, dtype=jnp.int32)[None, None, :]).astype(jnp.int32)
    before = jnp.cumsum(onehot, axis=1) - onehot
    position = jnp.sum(onehot * before, axis=2)
    source = jnp.arange(devices, dtype=jnp.int32)[:, None]
    slot_index = ((route_flat * devices + source) * CAP + position).reshape(-1).astype(jnp.int32)
    total_slots = EXPERTS * devices * CAP
    pair_ids = jnp.arange(TOKENS * TOPK, dtype=jnp.int32)
    slot_token = jnp.zeros((total_slots,), jnp.int32).at[slot_index].set(pair_ids // TOPK)
    slot_pair = jnp.zeros((total_slots,), jnp.int32).at[slot_index].set(pair_ids)
    slot_alive = jnp.zeros((total_slots,), jnp.float32).at[slot_index].set(1.0)
    expert_cot = (gates[:, :, None] * d_out.astype(jnp.float32)[:, None, :]).astype(jnp.bfloat16).reshape(TOKENS * TOPK, D)

    def one_expert(inputs):
        return expert_pass(inputs + (tokens, expert_cot))

    outs_all, parts_all, grad_gate, grad_up, grad_down = lax.map(one_expert, (w_gate, w_up, w_down, slot_token.reshape(EXPERTS, -1), slot_pair.reshape(EXPERTS, -1), slot_alive.reshape(EXPERTS, -1)))
    expert_out = outs_all.reshape(-1, D)[slot_index].reshape(TOKENS, TOPK, D)
    d_part = parts_all.reshape(-1, D)[slot_index].reshape(TOKENS, TOPK, D)
    mixture = jnp.sum(gates[:, :, None] * expert_out.astype(jnp.float32), axis=1).astype(jnp.bfloat16)
    d_gates = jnp.einsum('td,tkd->tk', d_out.astype(jnp.float32), expert_out.astype(jnp.float32))
    d_tokens = jnp.sum(d_part.astype(jnp.float32), axis=1).astype(jnp.bfloat16)
    slots = jnp.arange(EXPERTS, dtype=jnp.int32)
    half_axis = EXPERTS // 2
    partner = jnp.where(slots < half_axis, slots + half_axis, slots - half_axis)
    placed = jnp.where(swap_flags == 1, partner, slots).astype(jnp.int32)
    return mixture, d_tokens, d_gates, grad_gate[placed], grad_up[placed], grad_down[placed]
```

```python
import jax
import jax.numpy as jnp
from jax import lax
from jax.sharding import Mesh, PartitionSpec as P

N_Z, N_X, N_CORE = 8, 4, 2
PLANE = ("x", "core")
BF16, F32 = jnp.bfloat16, jnp.float32


def dot(left, right, lc=1, rc=0):
    return lax.dot_general(left, right, (((lc,), (rc,)), ((), ())), preferred_element_type=F32)


def split3(value):
    first = lax.reduce_precision(value, 8, 7)
    second = lax.reduce_precision(value - first, 8, 7)
    third = value - first - second
    return [part.astype(BF16) for part in (first, second, third)]


def padded(parts, width):
    used = sum(p.shape[1] for p in parts)
    return jnp.concatenate(parts + [jnp.zeros((parts[0].shape[0], width - used), BF16)], axis=1)


def on_device(tokens, routes, gates, w_gate, w_up, w_down, swap_flags, d_out):
    tok_count, model_width = tokens.shape
    top_count = routes.shape[1]
    plane = N_X * N_CORE
    experts = N_Z * plane
    capacity = min(tok_count, (3 * tok_count * top_count + 2 * experts - 1) // (2 * experts))
    column = N_Z * tok_count
    per_expert = N_Z * capacity
    slots = plane * per_expert
    z_index = lax.axis_index("z")
    own_index = (z_index * N_X + lax.axis_index("x")) * N_CORE + lax.axis_index("core")
    own_flag = swap_flags[own_index]
    gate_mat, up_mat, down_mat = w_gate[0], w_up[0], w_down[0]

    meta = padded([routes.astype(BF16)] + split3(gates), 128)
    tok_meta = lax.all_gather(jnp.concatenate([tokens, meta], axis=1), "z", tiled=True)
    dout_col = lax.all_gather(d_out, "z", tiled=True)
    tok_col = tok_meta[:, :model_width]
    meta_col = tok_meta[:, model_width : model_width + 4 * top_count].astype(F32)
    routes_col = meta_col[:, :top_count].astype(jnp.int32) - z_index * plane
    gates_col = (
        meta_col[:, top_count : 2 * top_count]
        + meta_col[:, 2 * top_count : 3 * top_count]
        + meta_col[:, 3 * top_count :]
    )

    named = routes_col[:, None, :] == jnp.arange(plane, dtype=jnp.int32)[None, :, None]
    member = jnp.any(named, axis=2)
    gate_of = jnp.sum(jnp.where(named, gates_col[:, None, :], 0.0), axis=2)
    row = jnp.arange(column, dtype=jnp.int32)
    earlier = (row[:, None] > row[None, :]) & (
        row[:, None] // tok_count == row[None, :] // tok_count
    )
    position = dot(earlier.astype(BF16), member.astype(BF16)).astype(jnp.int32)
    slot_of = jnp.where(
        member,
        jnp.arange(plane, dtype=jnp.int32)[None, :] * per_expert
        + (row // tok_count)[:, None] * capacity
        + position,
        -1,
    )
    slot_ids = jnp.arange(slots, dtype=jnp.int32).reshape(plane, per_expert)
    pick = slot_of.T[:, None, :] == slot_ids[:, :, None]
    slot_gate = jnp.sum(jnp.where(pick, gate_of.T[:, None, :], 0.0), axis=2).reshape(slots, 1)
    pick = pick.astype(BF16).reshape(slots, column)

    def to_plane(rows):
        return lax.all_to_all(
            rows.reshape(plane, per_expert, -1), PLANE, split_axis=0, concat_axis=0, tiled=True
        ).reshape(slots, -1)

    def to_column(rows):
        return lax.all_to_all(
            rows.reshape(N_Z, tok_count, -1), "z", split_axis=0, concat_axis=0, tiled=True
        )

    rows_in = to_plane(dot(pick, tok_col).astype(BF16))
    cot_rows = to_plane((slot_gate * dot(pick, dout_col)).astype(BF16))

    pre_gate = dot(rows_in, gate_mat)
    pre_up = dot(rows_in, up_mat)
    logistic = jax.nn.sigmoid(pre_gate)
    activated = pre_gate * logistic
    hidden = (activated * pre_up).astype(BF16)
    result = dot(hidden, down_mat).astype(BF16)
    d_hidden = dot(cot_rows, down_mat, 1, 1)
    grad_gate_pre = (d_hidden * pre_up * logistic * (1.0 + pre_gate * (1.0 - logistic))).astype(
        BF16
    )
    grad_up_pre = (d_hidden * activated).astype(BF16)
    d_rows = (dot(grad_gate_pre, gate_mat, 1, 1) + dot(grad_up_pre, up_mat, 1, 1)).astype(BF16)

    swap = [(i, i ^ (N_Z // 2)) for i in range(N_Z)]

    def placed(left, right):
        partial = dot(left, right, 0, 0).astype(BF16)
        own = lax.psum_scatter(partial, "dp", scatter_dimension=0, tiled=True)
        other = lax.ppermute(own, "z", swap)
        return jnp.where(own_flag == 1, other, own)

    g_down = placed(cot_rows, hidden).T[None]
    g_gate = placed(rows_in, grad_gate_pre)[None]
    g_up = placed(rows_in, grad_up_pre)[None]

    out_rows = to_plane(result)
    weight = jnp.where(
        pick == 1, jnp.broadcast_to(slot_gate, pick.shape), 0.0
    )
    weight_hi = lax.reduce_precision(weight, 8, 7)
    weight_lo = (weight - weight_hi).astype(BF16)
    mix_part = dot(weight_hi.astype(BF16), out_rows, 0, 0) + dot(weight_lo, out_rows, 0, 0)
    cross = dot(dout_col, out_rows, 1, 1)
    slot_expert = jnp.arange(slots, dtype=jnp.int32) // per_expert
    cross = cross * pick.T.astype(F32)
    dg_part = jnp.sum(
        jnp.where(routes_col[:, :, None] == slot_expert[None, None, :], cross[:, None, :], 0.0),
        axis=2,
    )
    parts = to_column(
        jnp.concatenate([mix_part.astype(BF16), padded(split3(dg_part), 128)], axis=1)
    )
    mixture = jnp.sum(parts[:, :, :model_width].astype(F32), axis=0).astype(BF16)
    dg_sum = jnp.sum(parts[:, :, model_width : model_width + 3 * top_count].astype(F32), axis=0)
    d_gates = (
        dg_sum[:, :top_count]
        + dg_sum[:, top_count : 2 * top_count]
        + dg_sum[:, 2 * top_count :]
    )
    back_rows = to_plane(d_rows)
    d_tokens = jnp.sum(
        to_column(dot(pick, back_rows, 0, 0).astype(BF16)).astype(F32), axis=0
    ).astype(BF16)
    return (mixture, d_tokens, d_gates, g_gate, g_up, g_down)


def solution(mesh):
    fine = Mesh(mesh.devices.reshape(-1, N_Z, N_X, N_CORE), ("dp", "z", "x", "core"))
    every = ("dp", "z", "x", "core")
    expert = ("z", "x", "core")
    return jax.shard_map(
        on_device,
        mesh=fine,
        in_specs=(
            P(every, None),
            P(every, None),
            P(every, None),
            P(expert, None, None),
            P(expert, None, None),
            P(expert, None, None),
            P(),
            P(every, None),
        ),
        out_specs=(
            P(every, None),
            P(every, None),
            P(every, None),
            P(expert, "dp", None),
            P(expert, "dp", None),
            P(expert, None, "dp"),
        ),
        check_vma=False,
    )
```

```python
import jax
import jax.numpy as jnp
from jax import lax
from jax.sharding import Mesh, PartitionSpec as P


N_Z, N_X, N_CORE = 8, 4, 2
PLANE = ("x", "core")
BF16, F32 = jnp.bfloat16, jnp.float32


def dot(left, right, lc=1, rc=0):
    return lax.dot_general(left, right, (((lc,), (rc,)), ((), ())), preferred_element_type=F32)


def split3(value):
    first = lax.reduce_precision(value, 8, 7)
    second = lax.reduce_precision(value - first, 8, 7)
    third = value - first - second
    return [part.astype(BF16) for part in (first, second, third)]


def padded(parts, width):
    used = sum(p.shape[1] for p in parts)
    return jnp.concatenate(parts + [jnp.zeros((parts[0].shape[0], width - used), BF16)], axis=1)


def on_device(tokens, routes, gates, w_gate, w_up, w_down, swap_flags, d_out):
    tok_count, model_width = tokens.shape
    top_count = routes.shape[1]
    plane = N_X * N_CORE
    experts = N_Z * plane
    capacity = min(tok_count, (3 * tok_count * top_count + 2 * experts - 1) // (2 * experts))
    column = N_Z * tok_count
    per_expert = N_Z * capacity
    slots = plane * per_expert
    z_index = lax.axis_index("z")
    own_index = (z_index * N_X + lax.axis_index("x")) * N_CORE + lax.axis_index("core")
    own_flag = swap_flags[own_index]
    gate_mat, up_mat, down_mat = w_gate[0], w_up[0], w_down[0]

    meta = padded([routes.astype(BF16)] + split3(gates), 128)
    gathered = lax.all_gather(jnp.concatenate([tokens, d_out, meta], axis=1), "z", tiled=True)
    tok_col = gathered[:, :model_width]
    dout_col = gathered[:, model_width : 2 * model_width]
    meta_col = gathered[:, 2 * model_width : 2 * model_width + 4 * top_count].astype(F32)
    routes_col = meta_col[:, :top_count].astype(jnp.int32)
    gates_col = (
        meta_col[:, top_count : 2 * top_count]
        + meta_col[:, 2 * top_count : 3 * top_count]
        + meta_col[:, 3 * top_count :]
    )

    block = jnp.arange(experts, dtype=jnp.int32)
    block_expert = block % N_Z * plane + block // N_Z
    sent = jnp.any(routes[:, None, :] == block_expert[None, :, None], axis=2)
    own_row = jnp.arange(tok_count, dtype=jnp.int32)
    own_position = dot(
        (own_row[:, None] > own_row[None, :]).astype(BF16), sent.astype(BF16)
    ).astype(jnp.int32)
    own_pick = jnp.where(sent, own_position, -1).T[:, None, :] == jnp.arange(
        capacity, dtype=jnp.int32
    )[None, :, None]
    own_pick = own_pick.reshape(slots, tok_count).astype(BF16)
    outbound = dot(own_pick, tokens).astype(BF16).reshape(experts, capacity, model_width)
    rows_in = lax.all_to_all(
        outbound, ("x", "core", "z"), split_axis=0, concat_axis=0, tiled=True
    ).reshape(slots, model_width)

    row = jnp.arange(column, dtype=jnp.int32)
    earlier = (
        (row[:, None] > row[None, :])
        & (row[:, None] // tok_count == row[None, :] // tok_count)
    ).astype(BF16)
    slot_ids = jnp.arange(slots, dtype=jnp.int32).reshape(plane, per_expert)

    def selection(ids):
        named = routes_col[:, None, :] == ids[None, :, None]
        member = jnp.any(named, axis=2)
        gate_of = jnp.sum(jnp.where(named, gates_col[:, None, :], 0.0), axis=2)
        position = dot(earlier, member.astype(BF16)).astype(jnp.int32)
        slot_of = jnp.where(
            member,
            jnp.arange(plane, dtype=jnp.int32)[None, :] * per_expert
            + (row // tok_count)[:, None] * capacity
            + position,
            -1,
        )
        pick = slot_of.T[:, None, :] == slot_ids[:, :, None]
        slot_gate = jnp.sum(jnp.where(pick, gate_of.T[:, None, :], 0.0), axis=2)
        return pick.astype(BF16).reshape(slots, column), slot_gate.reshape(slots, 1)

    def to_plane(rows):
        rows = rows.reshape(plane, per_expert, -1)
        rows = lax.all_to_all(rows, PLANE, split_axis=0, concat_axis=0, tiled=True)
        return rows.reshape(slots, -1)

    def to_column(rows):
        rows = rows.reshape(N_Z, tok_count, -1)
        return lax.all_to_all(rows, "z", split_axis=0, concat_axis=0, tiled=True)

    def token_rows(pick):
        rows = dot(pick, tok_col).astype(BF16)
        return to_plane(rows)

    def cot_pairs(pick, slot_gate):
        rows = (slot_gate * dot(pick, dout_col)).astype(BF16)
        return to_plane(rows)

    plane_ids = z_index * plane + jnp.arange(plane, dtype=jnp.int32)
    pick, slot_gate = selection(plane_ids)
    cot_rows = cot_pairs(pick, slot_gate)

    plane_flags = lax.dynamic_slice(swap_flags, (z_index * plane,), (plane,))
    placed_pick, placed_gate = selection(
        jnp.where(plane_flags == 1, plane_ids ^ (experts // 2), plane_ids)
    )
    placed_cot = cot_pairs(placed_pick, placed_gate)
    placed_tok = token_rows(placed_pick)

    pre_gate = dot(rows_in, gate_mat)
    pre_up = dot(rows_in, up_mat)
    logistic = jax.nn.sigmoid(pre_gate)
    activated = pre_gate * logistic
    hidden = (activated * pre_up).astype(BF16)
    _, cot_rows = lax.optimization_barrier((hidden, cot_rows))
    d_hidden = dot(cot_rows, down_mat, 1, 1)
    grad_gate_pre = (d_hidden * pre_up * logistic * (1.0 + pre_gate * (1.0 - logistic))).astype(
        BF16
    )
    grad_up_pre = (d_hidden * activated).astype(BF16)
    result = dot(hidden, down_mat).astype(BF16)
    d_rows = (dot(grad_gate_pre, gate_mat, 1, 1) + dot(grad_up_pre, up_mat, 1, 1)).astype(BF16)

    def placed(own):
        other = lax.ppermute(own, "z", [(i, i ^ (N_Z // 2)) for i in range(N_Z)])
        return jnp.where(own_flag == 1, other, own)

    def reduced(left, right):
        partial = dot(left, right, 0, 0).astype(BF16)
        return lax.psum_scatter(partial, "dp", scatter_dimension=0, tiled=True)

    g_down = reduced(placed_cot, placed(hidden)).T[None]
    g_gate = reduced(placed_tok, placed(grad_gate_pre))[None]
    g_up = reduced(placed_tok, placed(grad_up_pre))[None]

    out_rows = to_plane(result)
    weight = jnp.where(
        pick == 1, jnp.broadcast_to(slot_gate, pick.shape), 0.0
    )
    weight_hi = lax.reduce_precision(weight, 8, 7)
    weight_lo = (weight - weight_hi).astype(BF16)
    mix_part = dot(weight_hi.astype(BF16), out_rows, 0, 0) + dot(weight_lo, out_rows, 0, 0)
    cross = dot(dout_col, out_rows, 1, 1)
    slot_expert = z_index * plane + jnp.arange(slots, dtype=jnp.int32) // per_expert
    cross = cross * pick.T.astype(F32)
    dg_part = jnp.sum(
        jnp.where(routes_col[:, :, None] == slot_expert[None, None, :], cross[:, None, :], 0.0),
        axis=2,
    )
    parts = to_column(
        jnp.concatenate([mix_part.astype(BF16), padded(split3(dg_part), 128)], axis=1),
    )
    mixture = jnp.sum(parts[:, :, :model_width].astype(F32), axis=0).astype(BF16)
    dg_sum = jnp.sum(parts[:, :, model_width : model_width + 3 * top_count].astype(F32), axis=0)
    d_gates = (
        dg_sum[:, :top_count]
        + dg_sum[:, top_count : 2 * top_count]
        + dg_sum[:, 2 * top_count :]
    )
    back_rows = to_plane(d_rows)
    d_tokens = jnp.sum(
        to_column(dot(pick, back_rows, 0, 0).astype(BF16)).astype(F32), axis=0
    ).astype(BF16)
    return (mixture, d_tokens, d_gates, g_gate, g_up, g_down)


def solution(mesh):
    fine = Mesh(mesh.devices.reshape(-1, N_Z, N_X, N_CORE), ("dp", "z", "x", "core"))
    every = ("dp", "z", "x", "core")
    expert = ("z", "x", "core")
    return jax.shard_map(
        on_device,
        mesh=fine,
        in_specs=(
            P(every, None),
            P(every, None),
            P(every, None),
            P(expert, None, None),
            P(expert, None, None),
            P(expert, None, None),
            P(),
            P(every, None),
        ),
        out_specs=(
            P(every, None),
            P(every, None),
            P(every, None),
            P(expert, "dp", None),
            P(expert, "dp", None),
            P(expert, None, "dp"),
        ),
        check_vma=False,
    )
```

```python
import jax
import jax.numpy as jnp
from jax import lax
from jax.sharding import Mesh, PartitionSpec as P


N_Z, N_X, N_CORE = 8, 4, 2
PLANE = ("x", "core")
BF16, F32 = jnp.bfloat16, jnp.float32


def dot(left, right, lc=1, rc=0):
    return lax.dot_general(left, right, (((lc,), (rc,)), ((), ())), preferred_element_type=F32)


def split3(value):
    first = lax.reduce_precision(value, 8, 7)
    second = lax.reduce_precision(value - first, 8, 7)
    third = value - first - second
    return [part.astype(BF16) for part in (first, second, third)]


def padded(parts, width):
    used = sum(p.shape[1] for p in parts)
    return jnp.concatenate(parts + [jnp.zeros((parts[0].shape[0], width - used), BF16)], axis=1)


def on_device(tokens, routes, gates, w_gate, w_up, w_down, swap_flags, d_out):
    tok_count, model_width = tokens.shape
    top_count = routes.shape[1]
    plane = N_X * N_CORE
    experts = N_Z * plane
    capacity = min(tok_count, (3 * tok_count * top_count + 2 * experts - 1) // (2 * experts))
    column = N_Z * tok_count
    per_expert = N_Z * capacity
    slots = plane * per_expert
    z_index = lax.axis_index("z")
    own_index = (z_index * N_X + lax.axis_index("x")) * N_CORE + lax.axis_index("core")
    own_flag = swap_flags[own_index]
    gate_mat, up_mat, down_mat = w_gate[0], w_up[0], w_down[0]

    meta = padded([routes.astype(BF16)] + split3(gates), 128)
    gathered = lax.all_gather(
        jnp.concatenate([tokens, d_out, meta], axis=1), ("z", "x", "core"), tiled=True
    )

    def parts_of(block):
        info = block[:, 2 * model_width : 2 * model_width + 4 * top_count].astype(F32)
        named, first, second, third = [
            info[:, i * top_count : (i + 1) * top_count] for i in range(4)
        ]
        return block[:, :model_width], block[:, model_width : 2 * model_width], named, (
            first + second + third
        )

    tok_all, dout_all, routes_all, gates_all = parts_of(gathered)
    own_row = jnp.arange(tok_count, dtype=jnp.int32)
    before = (own_row[:, None] < own_row[None, :]).astype(BF16)
    source = jnp.arange(experts, dtype=jnp.int32)
    first_slot = ((source % plane) * N_Z + source // plane) * capacity
    slot_ids = jnp.arange(slots, dtype=jnp.int32)

    def rows_of(expert):
        named = routes_all == expert.astype(F32)
        member = jnp.any(named, axis=1)
        gate_of = jnp.sum(jnp.where(named, gates_all, 0.0), axis=1)
        spread = member.reshape(experts, tok_count)
        position = dot(spread.astype(BF16), before).astype(jnp.int32)
        slot_of = jnp.where(spread, first_slot[:, None] + position, -1).reshape(1, -1)
        pick = slot_of == slot_ids[:, None]
        slot_gate = jnp.sum(jnp.where(pick, gate_of[None, :], 0.0), axis=1, keepdims=True)
        return pick.astype(BF16), slot_gate

    placed_index = jnp.where(own_flag == 1, own_index ^ (experts // 2), own_index)
    home_pick, home_gate = rows_of(own_index)
    rows_in = dot(home_pick, tok_all).astype(BF16)
    cot_rows = (home_gate * dot(home_pick, dout_all)).astype(BF16)
    placed_pick, placed_gate = rows_of(placed_index)
    placed_cot = (placed_gate * dot(placed_pick, dout_all)).astype(BF16)
    placed_tok = dot(placed_pick, tok_all).astype(BF16)
    placed_cot = lax.optimization_barrier(placed_cot)

    column_block = lax.dynamic_index_in_dim(
        gathered.reshape(N_Z, plane, tok_count, -1), own_index % plane, axis=1, keepdims=False
    ).reshape(column, -1)
    _, dout_col, routes_col, gates_col = parts_of(column_block)
    plane_ids = z_index * plane + jnp.arange(plane, dtype=jnp.int32)
    row = jnp.arange(column, dtype=jnp.int32)
    earlier = (
        (row[:, None] > row[None, :])
        & (row[:, None] // tok_count == row[None, :] // tok_count)
    ).astype(BF16)
    named = routes_col[:, None, :] == plane_ids.astype(F32)[None, :, None]
    member = jnp.any(named, axis=2)
    gate_of = jnp.sum(jnp.where(named, gates_col[:, None, :], 0.0), axis=2)
    slot_of = jnp.where(
        member,
        jnp.arange(plane, dtype=jnp.int32)[None, :] * per_expert
        + (row // tok_count)[:, None] * capacity
        + dot(earlier, member.astype(BF16)).astype(jnp.int32),
        -1,
    )
    pick = slot_of.T[:, None, :] == slot_ids.reshape(plane, per_expert)[:, :, None]
    slot_gate = jnp.sum(jnp.where(pick, gate_of.T[:, None, :], 0.0), axis=2).reshape(slots, 1)
    pick = pick.astype(BF16).reshape(slots, column)

    def to_plane(rows):
        rows = rows.reshape(plane, per_expert, -1)
        rows = lax.all_to_all(rows, PLANE, split_axis=0, concat_axis=0, tiled=True)
        return rows.reshape(slots, -1)

    def to_column(rows):
        rows = rows.reshape(N_Z, tok_count, -1)
        return lax.all_to_all(rows, "z", split_axis=0, concat_axis=0, tiled=True)

    pre_gate = dot(rows_in, gate_mat)
    pre_up = dot(rows_in, up_mat)
    logistic = jax.nn.sigmoid(pre_gate)
    activated = pre_gate * logistic
    hidden = (activated * pre_up).astype(BF16)
    _, cot_rows = lax.optimization_barrier((hidden, cot_rows))
    d_hidden = dot(cot_rows, down_mat, 1, 1)
    grad_gate_pre = (d_hidden * pre_up * logistic * (1.0 + pre_gate * (1.0 - logistic))).astype(
        BF16
    )
    grad_up_pre = (d_hidden * activated).astype(BF16)
    result = dot(hidden, down_mat).astype(BF16)
    d_rows = (dot(grad_gate_pre, gate_mat, 1, 1) + dot(grad_up_pre, up_mat, 1, 1)).astype(BF16)

    def placed(own):
        other = lax.ppermute(own, "z", [(i, i ^ (N_Z // 2)) for i in range(N_Z)])
        return jnp.where(own_flag == 1, other, own)

    def reduced(left, right):
        partial = dot(left, right, 0, 0).astype(BF16)
        return lax.psum_scatter(partial, "dp", scatter_dimension=0, tiled=True)

    g_down = reduced(placed_cot, placed(hidden)).T[None]
    g_up = reduced(placed_tok, placed(grad_up_pre))[None]
    placed_gate_pre = placed(grad_gate_pre)
    dp_index, dp_count = lax.axis_index("dp"), lax.axis_size("dp")
    share = model_width // dp_count
    partial = dot(placed_tok, placed_gate_pre, 0, 0).astype(BF16)
    total = 0.0
    for step in range(dp_count):
        block = lax.dynamic_slice(
            partial, ((dp_index + step) % dp_count * share, 0), (share, partial.shape[1])
        )
        if step:
            block = lax.ppermute(block, "dp", [(i, (i + step) % dp_count) for i in range(dp_count)])
        total = total + block.astype(F32)
    g_gate = total.astype(BF16)[None]

    out_rows = to_plane(result)
    weight = jnp.where(
        pick == 1, jnp.broadcast_to(slot_gate, pick.shape), 0.0
    )
    weight_hi = lax.reduce_precision(weight, 8, 7)
    weight_lo = (weight - weight_hi).astype(BF16)
    mix_part = dot(weight_hi.astype(BF16), out_rows, 0, 0) + dot(weight_lo, out_rows, 0, 0)
    cross = dot(dout_col, out_rows, 1, 1)
    slot_expert = z_index * plane + jnp.arange(slots, dtype=jnp.int32) // per_expert
    cross = cross * pick.T.astype(F32)
    dg_part = jnp.sum(
        jnp.where(routes_col[:, :, None] == slot_expert.astype(F32)[None, None, :], cross[:, None, :], 0.0),
        axis=2,
    )
    parts = to_column(
        jnp.concatenate([mix_part.astype(BF16), padded(split3(dg_part), 128)], axis=1),
    )
    mixture = jnp.sum(parts[:, :, :model_width].astype(F32), axis=0).astype(BF16)
    dg_sum = jnp.sum(parts[:, :, model_width : model_width + 3 * top_count].astype(F32), axis=0)
    d_gates = (
        dg_sum[:, :top_count]
        + dg_sum[:, top_count : 2 * top_count]
        + dg_sum[:, 2 * top_count :]
    )
    back_rows = to_plane(d_rows)
    d_tokens = jnp.sum(
        to_column(dot(pick, back_rows, 0, 0).astype(BF16)).astype(F32), axis=0
    ).astype(BF16)
    return (mixture, d_tokens, d_gates, g_gate, g_up, g_down)


def solution(mesh):
    fine = Mesh(mesh.devices.reshape(-1, N_Z, N_X, N_CORE), ("dp", "z", "x", "core"))
    every = ("dp", "z", "x", "core")
    expert = ("z", "x", "core")
    return jax.shard_map(
        on_device,
        mesh=fine,
        in_specs=(
            P(every, None),
            P(every, None),
            P(every, None),
            P(expert, None, None),
            P(expert, None, None),
            P(expert, None, None),
            P(),
            P(every, None),
        ),
        out_specs=(
            P(every, None),
            P(every, None),
            P(every, None),
            P(expert, "dp", None),
            P(expert, "dp", None),
            P(expert, None, "dp"),
        ),
        check_vma=False,
    )
```

```python
import jax
import jax.numpy as jnp
from jax import lax
from jax.sharding import Mesh, PartitionSpec as P


N_Z, N_X, N_CORE = 8, 4, 2
PLANE = ("x", "core")
BF16, F32 = jnp.bfloat16, jnp.float32


def dot(left, right, lc=1, rc=0):
    return lax.dot_general(left, right, (((lc,), (rc,)), ((), ())), preferred_element_type=F32)


def split3(value):
    first = lax.reduce_precision(value, 8, 7)
    second = lax.reduce_precision(value - first, 8, 7)
    third = value - first - second
    return [part.astype(BF16) for part in (first, second, third)]


def padded(parts, width):
    used = sum(p.shape[1] for p in parts)
    return jnp.concatenate(parts + [jnp.zeros((parts[0].shape[0], width - used), BF16)], axis=1)


def on_device(tokens, routes, gates, w_gate, w_up, w_down, swap_flags, d_out):
    tok_count, model_width = tokens.shape
    top_count = routes.shape[1]
    plane = N_X * N_CORE
    experts = N_Z * plane
    capacity = min(tok_count, (3 * tok_count * top_count + 2 * experts - 1) // (2 * experts))
    column = N_Z * tok_count
    per_expert = N_Z * capacity
    slots = plane * per_expert
    z_index = lax.axis_index("z")
    own_index = (z_index * N_X + lax.axis_index("x")) * N_CORE + lax.axis_index("core")
    own_flag = swap_flags[own_index]
    gate_mat, up_mat, down_mat = w_gate[0], w_up[0], w_down[0]

    meta = padded([routes.astype(BF16)] + split3(gates), 128)
    gathered = lax.all_gather(jnp.concatenate([tokens, d_out, meta], axis=1), "z", tiled=True)
    tok_col = gathered[:, :model_width]
    dout_col = gathered[:, model_width : 2 * model_width]
    meta_col = gathered[:, 2 * model_width : 2 * model_width + 4 * top_count].astype(F32)
    routes_col = meta_col[:, :top_count].astype(jnp.int32)
    gates_col = (
        meta_col[:, top_count : 2 * top_count]
        + meta_col[:, 2 * top_count : 3 * top_count]
        + meta_col[:, 3 * top_count :]
    )
    row = jnp.arange(column, dtype=jnp.int32)
    earlier = (
        (row[:, None] > row[None, :])
        & (row[:, None] // tok_count == row[None, :] // tok_count)
    ).astype(BF16)
    slot_ids = jnp.arange(slots, dtype=jnp.int32).reshape(plane, per_expert)

    def selection(ids, routes_col):
        named = routes_col[:, None, :] == ids[None, :, None]
        member = jnp.any(named, axis=2)
        gate_of = jnp.sum(jnp.where(named, gates_col[:, None, :], 0.0), axis=2)
        position = dot(earlier, member.astype(BF16)).astype(jnp.int32)
        slot_of = jnp.where(
            member,
            jnp.arange(plane, dtype=jnp.int32)[None, :] * per_expert
            + (row // tok_count)[:, None] * capacity
            + position,
            -1,
        )
        pick = slot_of.T[:, None, :] == slot_ids[:, :, None]
        slot_gate = jnp.sum(jnp.where(pick, gate_of.T[:, None, :], 0.0), axis=2)
        return pick.astype(BF16).reshape(slots, column), slot_gate.reshape(slots, 1)

    def to_plane(rows):
        rows = rows.reshape(plane, per_expert, -1)
        rows = lax.all_to_all(rows, PLANE, split_axis=0, concat_axis=0, tiled=True)
        return rows.reshape(slots, -1)

    def to_column(rows):
        rows = rows.reshape(N_Z, tok_count, -1)
        return lax.all_to_all(rows, "z", split_axis=0, concat_axis=0, tiled=True)

    def token_rows(pick):
        rows = dot(pick, tok_col).astype(BF16)
        return to_plane(rows)

    def cot_pairs(pick, slot_gate):
        rows = (slot_gate * dot(pick, dout_col)).astype(BF16)
        return to_plane(rows)

    plane_ids = z_index * plane + jnp.arange(plane, dtype=jnp.int32)
    pick, slot_gate = selection(plane_ids, routes_col)
    rows_in = token_rows(pick)
    cot_rows = cot_pairs(pick, slot_gate)

    plane_flags = lax.dynamic_slice(swap_flags, (z_index * plane,), (plane,))
    later_routes, _ = lax.optimization_barrier((routes_col, rows_in))
    placed_pick, _ = selection(
        jnp.where(plane_flags == 1, plane_ids ^ (experts // 2), plane_ids), later_routes
    )
    placed_tok = token_rows(placed_pick)

    pre_gate = dot(rows_in, gate_mat)
    pre_up = dot(rows_in, up_mat)
    logistic = jax.nn.sigmoid(pre_gate)
    activated = pre_gate * logistic
    hidden = (activated * pre_up).astype(BF16)
    _, cot_rows = lax.optimization_barrier((hidden, cot_rows))
    d_hidden = dot(cot_rows, down_mat, 1, 1)
    grad_gate_pre = (d_hidden * pre_up * logistic * (1.0 + pre_gate * (1.0 - logistic))).astype(
        BF16
    )
    grad_up_pre = (d_hidden * activated).astype(BF16)
    result = dot(hidden, down_mat).astype(BF16)
    d_rows = (
        dot(grad_gate_pre, gate_mat, 1, 1) + dot(grad_up_pre, up_mat, 1, 1)
    ).astype(BF16)

    def placed(own):
        other = lax.ppermute(own, "z", [(i, i ^ (N_Z // 2)) for i in range(N_Z)])
        return jnp.where(own_flag == 1, other, own)

    def reduced(left, right):
        partial = dot(left, right, 0, 0).astype(BF16)
        return lax.psum_scatter(partial, "dp", scatter_dimension=0, tiled=True)

    g_down = placed(reduced(cot_rows, hidden)).T[None]
    g_gate = reduced(placed_tok, placed(grad_gate_pre))[None]
    g_up = reduced(placed_tok, placed(grad_up_pre))[None]

    out_rows = to_plane(result)
    weight = jnp.where(
        pick == 1, jnp.broadcast_to(slot_gate, pick.shape), 0.0
    )
    weight_hi = lax.reduce_precision(weight, 8, 7)
    weight_lo = (weight - weight_hi).astype(BF16)
    mix_part = dot(weight_hi.astype(BF16), out_rows, 0, 0) + dot(weight_lo, out_rows, 0, 0)
    cross = dot(dout_col, out_rows, 1, 1)
    slot_expert = z_index * plane + jnp.arange(slots, dtype=jnp.int32) // per_expert
    cross = cross * pick.T.astype(F32)
    dg_part = jnp.sum(
        jnp.where(routes_col[:, :, None] == slot_expert[None, None, :], cross[:, None, :], 0.0),
        axis=2,
    )
    parts = to_column(
        jnp.concatenate([mix_part.astype(BF16), padded(split3(dg_part), 128)], axis=1),
    )
    mixture = jnp.sum(parts[:, :, :model_width].astype(F32), axis=0).astype(BF16)
    dg_sum = jnp.sum(parts[:, :, model_width : model_width + 3 * top_count].astype(F32), axis=0)
    d_gates = (
        dg_sum[:, :top_count]
        + dg_sum[:, top_count : 2 * top_count]
        + dg_sum[:, 2 * top_count :]
    )
    back_rows = to_plane(d_rows)
    d_tokens = jnp.sum(
        to_column(dot(pick, back_rows, 0, 0).astype(BF16)).astype(F32), axis=0
    ).astype(BF16)
    return (mixture, d_tokens, d_gates, g_gate, g_up, g_down)


def solution(mesh):
    fine = Mesh(mesh.devices.reshape(-1, N_Z, N_X, N_CORE), ("dp", "z", "x", "core"))
    every = ("dp", "z", "x", "core")
    expert = ("z", "x", "core")
    return jax.shard_map(
        on_device,
        mesh=fine,
        in_specs=(
            P(every, None),
            P(every, None),
            P(every, None),
            P(expert, None, None),
            P(expert, None, None),
            P(expert, None, None),
            P(),
            P(every, None),
        ),
        out_specs=(
            P(every, None),
            P(every, None),
            P(every, None),
            P(expert, "dp", None),
            P(expert, "dp", None),
            P(expert, None, "dp"),
        ),
        check_vma=False,
    )
```

```python
import jax
import jax.numpy as jnp
from jax import lax
from jax.sharding import Mesh, PartitionSpec as P


N_Z, N_X, N_CORE = 8, 4, 2
PLANE = ("x", "core")
BF16, F32 = jnp.bfloat16, jnp.float32


def dot(left, right, lc=1, rc=0):
    return lax.dot_general(left, right, (((lc,), (rc,)), ((), ())), preferred_element_type=F32)


def split3(value):
    first = lax.reduce_precision(value, 8, 7)
    second = lax.reduce_precision(value - first, 8, 7)
    third = value - first - second
    return [part.astype(BF16) for part in (first, second, third)]


def padded(parts, width):
    used = sum(p.shape[1] for p in parts)
    return jnp.concatenate(parts + [jnp.zeros((parts[0].shape[0], width - used), BF16)], axis=1)


def on_device(tokens, routes, gates, w_gate, w_up, w_down, swap_flags, d_out):
    tok_count, model_width = tokens.shape
    top_count = routes.shape[1]
    plane = N_X * N_CORE
    experts = N_Z * plane
    capacity = min(tok_count, (3 * tok_count * top_count + 2 * experts - 1) // (2 * experts))
    column = N_Z * tok_count
    per_expert = N_Z * capacity
    slots = plane * per_expert
    z_index = lax.axis_index("z")
    own_index = (z_index * N_X + lax.axis_index("x")) * N_CORE + lax.axis_index("core")
    own_flag = swap_flags[own_index]
    gate_mat, up_mat, down_mat = w_gate[0], w_up[0], w_down[0]

    meta = padded([routes.astype(BF16)] + split3(gates), 128)
    gathered = lax.all_gather(jnp.concatenate([tokens, d_out, meta], axis=1), "z", tiled=True)
    tok_col = gathered[:, :model_width]
    dout_col = gathered[:, model_width : 2 * model_width]
    meta_col = gathered[:, 2 * model_width : 2 * model_width + 4 * top_count].astype(F32)
    routes_col = meta_col[:, :top_count].astype(jnp.int32)
    row = jnp.arange(column, dtype=jnp.int32)
    earlier = (
        (row[:, None] > row[None, :])
        & (row[:, None] // tok_count == row[None, :] // tok_count)
    ).astype(BF16)
    slot_ids = jnp.arange(slots, dtype=jnp.int32)
    spread = (
        slot_ids[:, None] // per_expert == jnp.arange(plane, dtype=jnp.int32)[None, :]
    ).astype(BF16)
    slot_rank = (slot_ids % per_expert).astype(F32)[:, None]
    first_rank = (row // tok_count * capacity).astype(F32)[:, None]

    def selection(ids, routes_col):
        named = routes_col[:, None, :] == ids[None, :, None]
        member = jnp.any(named, axis=2)
        rank = jnp.where(member, first_rank + dot(earlier, member.astype(BF16)), -1.0)
        return (dot(spread, rank.astype(BF16), 1, 1) == slot_rank).astype(BF16), named

    def to_plane(rows):
        rows = rows.reshape(plane, per_expert, -1)
        rows = lax.all_to_all(rows, PLANE, split_axis=0, concat_axis=0, tiled=True)
        return rows.reshape(slots, -1)

    def to_column(rows):
        rows = rows.reshape(N_Z, tok_count, -1)
        return lax.all_to_all(rows, "z", split_axis=0, concat_axis=0, tiled=True)

    def token_rows(pick):
        rows = dot(pick, tok_col).astype(BF16)
        return to_plane(rows)

    def cot_pairs(pick, slot_gate):
        rows = (slot_gate * dot(pick, dout_col)).astype(BF16)
        return to_plane(rows)

    plane_ids = z_index * plane + jnp.arange(plane, dtype=jnp.int32)
    pick, named = selection(plane_ids, routes_col)
    rows_in = token_rows(pick)
    gate_parts = [
        jnp.sum(
            jnp.where(named, meta_col[:, None, i * top_count : (i + 1) * top_count], 0.0), axis=2
        ).astype(BF16)
        for i in range(1, 4)
    ]
    slot_gate = jnp.sum(
        dot(pick, jnp.concatenate(gate_parts, axis=1)) * jnp.tile(spread, (1, 3)).astype(F32),
        axis=1,
        keepdims=True,
    )
    cot_rows = cot_pairs(pick, slot_gate)

    plane_flags = lax.dynamic_slice(swap_flags, (z_index * plane,), (plane,))
    later_routes, _ = lax.optimization_barrier((routes_col, rows_in))
    placed_pick, _ = selection(
        jnp.where(plane_flags == 1, plane_ids ^ (experts // 2), plane_ids), later_routes
    )
    placed_tok = token_rows(placed_pick)

    pre_gate = dot(rows_in, gate_mat)
    pre_up = dot(rows_in, up_mat)
    logistic = jax.nn.sigmoid(pre_gate)
    activated = pre_gate * logistic
    hidden = (activated * pre_up).astype(BF16)
    _, cot_rows = lax.optimization_barrier((hidden, cot_rows))
    d_hidden = dot(cot_rows, down_mat, 1, 1)
    grad_gate_pre = (d_hidden * pre_up * logistic * (1.0 + pre_gate * (1.0 - logistic))).astype(
        BF16
    )
    grad_up_pre = (d_hidden * activated).astype(BF16)
    result = dot(hidden, down_mat).astype(BF16)
    d_rows = (
        dot(grad_gate_pre, gate_mat, 1, 1) + dot(grad_up_pre, up_mat, 1, 1)
    ).astype(BF16)

    def placed(own):
        other = lax.ppermute(own, "z", [(i, i ^ (N_Z // 2)) for i in range(N_Z)])
        return jnp.where(own_flag == 1, other, own)

    def reduced(left, right):
        partial = dot(left, right, 0, 0).astype(BF16)
        return lax.psum_scatter(partial, "dp", scatter_dimension=0, tiled=True)

    g_down = placed(reduced(cot_rows, hidden)).T[None]
    g_gate = reduced(placed_tok, placed(grad_gate_pre))[None]
    g_up = reduced(placed_tok, placed(grad_up_pre))[None]

    out_rows = to_plane(result)
    weight = jnp.where(pick == 1, jnp.broadcast_to(slot_gate, pick.shape), 0.0)
    weight_hi = lax.reduce_precision(weight, 8, 7)
    weight_lo = (weight - weight_hi).astype(BF16)
    mix_part = dot(weight_hi.astype(BF16), out_rows, 0, 0) + dot(weight_lo, out_rows, 0, 0)
    mix_part = mix_part.astype(BF16)
    cross = dot(dout_col, out_rows, 1, 1) * pick.T.astype(F32)
    slot_expert = z_index * plane + jnp.arange(slots, dtype=jnp.int32) // per_expert
    dg_part = jnp.sum(
        jnp.where(routes_col[:, :, None] == slot_expert[None, None, :], cross[:, None, :], 0.0),
        axis=2,
    )
    back_rows = to_plane(d_rows)
    dtok_part = dot(pick, back_rows, 0, 0).astype(BF16)
    parts = to_column(jnp.concatenate([mix_part, dtok_part, padded(split3(dg_part), 128)], axis=1))
    mixture = jnp.sum(parts[:, :, :model_width].astype(F32), axis=0).astype(BF16)
    d_tokens = jnp.sum(
        parts[:, :, model_width : 2 * model_width].astype(F32), axis=0
    ).astype(BF16)
    dg_sum = jnp.sum(
        parts[:, :, 2 * model_width : 2 * model_width + 3 * top_count].astype(F32), axis=0
    )
    d_gates = (
        dg_sum[:, :top_count]
        + dg_sum[:, top_count : 2 * top_count]
        + dg_sum[:, 2 * top_count :]
    )
    return (mixture, d_tokens, d_gates, g_gate, g_up, g_down)


def solution(mesh):
    fine = Mesh(mesh.devices.reshape(-1, N_Z, N_X, N_CORE), ("dp", "z", "x", "core"))
    every = ("dp", "z", "x", "core")
    expert = ("z", "x", "core")
    return jax.shard_map(
        on_device,
        mesh=fine,
        in_specs=(
            P(every, None),
            P(every, None),
            P(every, None),
            P(expert, None, None),
            P(expert, None, None),
            P(expert, None, None),
            P(),
            P(every, None),
        ),
        out_specs=(
            P(every, None),
            P(every, None),
            P(every, None),
            P(expert, "dp", None),
            P(expert, "dp", None),
            P(expert, None, "dp"),
        ),
        check_vma=False,
    )
```

```python
import jax
import jax.numpy as jnp
from jax import lax
from jax.sharding import Mesh, PartitionSpec as P


N_Z, N_X, N_CORE = 8, 4, 2
PLANE = ("x", "core")
BF16, F32 = jnp.bfloat16, jnp.float32


def dot(left, right, lc=1, rc=0):
    return lax.dot_general(left, right, (((lc,), (rc,)), ((), ())), preferred_element_type=F32)


def split3(value):
    first = lax.reduce_precision(value, 8, 7)
    second = lax.reduce_precision(value - first, 8, 7)
    third = value - first - second
    return [part.astype(BF16) for part in (first, second, third)]


def padded(parts, width):
    used = sum(p.shape[1] for p in parts)
    return jnp.concatenate(parts + [jnp.zeros((parts[0].shape[0], width - used), BF16)], axis=1)


def on_device(tokens, routes, gates, w_gate, w_up, w_down, swap_flags, d_out):
    tok_count, model_width = tokens.shape
    top_count = routes.shape[1]
    plane = N_X * N_CORE
    experts = N_Z * plane
    capacity = min(tok_count, (3 * tok_count * top_count + 2 * experts - 1) // (2 * experts))
    column = N_Z * tok_count
    per_expert = N_Z * capacity
    slots = plane * per_expert
    z_index = lax.axis_index("z")
    own_index = (z_index * N_X + lax.axis_index("x")) * N_CORE + lax.axis_index("core")
    own_flag = swap_flags[own_index]
    gate_mat, up_mat, down_mat = w_gate[0], w_up[0], w_down[0]

    meta = padded([routes.astype(BF16)] + split3(gates), 128)
    gathered = lax.all_gather(jnp.concatenate([tokens, d_out, meta], axis=1), "z", tiled=True)
    tok_col = gathered[:, :model_width]
    dout_col = gathered[:, model_width : 2 * model_width]
    meta_col = gathered[:, 2 * model_width : 2 * model_width + 4 * top_count].astype(F32)
    routes_col = meta_col[:, :top_count].astype(jnp.int32)
    row = jnp.arange(column, dtype=jnp.int32)
    earlier = (
        (row[:, None] > row[None, :])
        & (row[:, None] // tok_count == row[None, :] // tok_count)
    ).astype(BF16)
    slot_ids = jnp.arange(slots, dtype=jnp.int32)
    spread = (
        slot_ids[:, None] // per_expert == jnp.arange(plane, dtype=jnp.int32)[None, :]
    ).astype(BF16)
    slot_rank = (slot_ids % per_expert).astype(F32)[:, None]
    first_rank = (row // tok_count * capacity).astype(F32)[:, None]

    def selection(ids, routes_col):
        named = routes_col[:, None, :] == ids[None, :, None]
        member = jnp.any(named, axis=2)
        rank = jnp.where(member, first_rank + dot(earlier, member.astype(BF16)), -1.0)
        return (dot(spread, rank.astype(BF16), 1, 1) == slot_rank).astype(BF16), named

    def to_plane(rows):
        rows = rows.reshape(plane, per_expert, -1)
        rows = lax.all_to_all(rows, PLANE, split_axis=0, concat_axis=0, tiled=True)
        return rows.reshape(slots, -1)

    def to_column(rows):
        rows = rows.reshape(N_Z, tok_count, -1)
        return lax.all_to_all(rows, "z", split_axis=0, concat_axis=0, tiled=True)

    def token_rows(pick):
        rows = dot(pick, tok_col).astype(BF16)
        return to_plane(rows)

    def cot_pairs(pick, slot_gate):
        rows = (slot_gate * dot(pick, dout_col)).astype(BF16)
        return to_plane(rows)

    plane_ids = z_index * plane + jnp.arange(plane, dtype=jnp.int32)
    pick, named = selection(plane_ids, routes_col)
    rows_in = token_rows(pick)
    gate_parts = [
        jnp.sum(
            jnp.where(named, meta_col[:, None, i * top_count : (i + 1) * top_count], 0.0), axis=2
        ).astype(BF16)
        for i in range(1, 4)
    ]
    slot_gate = jnp.sum(
        dot(pick, jnp.concatenate(gate_parts, axis=1)) * jnp.tile(spread, (1, 3)).astype(F32),
        axis=1,
        keepdims=True,
    )
    cot_rows = cot_pairs(pick, slot_gate)

    plane_flags = lax.dynamic_slice(swap_flags, (z_index * plane,), (plane,))
    later_routes, _ = lax.optimization_barrier((routes_col, rows_in))
    placed_pick, _ = selection(
        jnp.where(plane_flags == 1, plane_ids ^ (experts // 2), plane_ids), later_routes
    )
    placed_tok = token_rows(placed_pick)

    pre_gate = dot(rows_in, gate_mat)
    pre_up = dot(rows_in, up_mat)
    logistic = jax.nn.sigmoid(pre_gate)
    activated = pre_gate * logistic
    hidden = (activated * pre_up).astype(BF16)
    _, cot_rows = lax.optimization_barrier((hidden, cot_rows))
    down_partial = dot(cot_rows, hidden, 0, 0).astype(BF16)
    down_partial, cot_rows = lax.optimization_barrier((down_partial, cot_rows))
    d_hidden = dot(cot_rows, down_mat, 1, 1)
    grad_gate_pre = (d_hidden * pre_up * logistic * (1.0 + pre_gate * (1.0 - logistic))).astype(
        BF16
    )
    grad_up_pre = (d_hidden * activated).astype(BF16)
    result = dot(hidden, down_mat).astype(BF16)
    d_rows = (
        dot(grad_gate_pre, gate_mat, 1, 1) + dot(grad_up_pre, up_mat, 1, 1)
    ).astype(BF16)

    def placed(own):
        other = lax.ppermute(own, "z", [(i, i ^ (N_Z // 2)) for i in range(N_Z)])
        return jnp.where(own_flag == 1, other, own)

    def reduced(partial):
        return lax.psum_scatter(partial, "dp", scatter_dimension=0, tiled=True)

    g_down = placed(reduced(down_partial)).T[None]
    placed_gate_pre = placed(grad_gate_pre)
    gate_partial = dot(placed_tok, placed_gate_pre, 0, 0).astype(BF16)
    g_gate = reduced(gate_partial)[None]
    placed_up_pre = placed(grad_up_pre)
    up_partial = dot(placed_tok, placed_up_pre, 0, 0).astype(BF16)
    g_up = reduced(up_partial)[None]

    out_rows = to_plane(result)
    weight = jnp.where(pick == 1, jnp.broadcast_to(slot_gate, pick.shape), 0.0)
    weight_hi = lax.reduce_precision(weight, 8, 7)
    weight_lo = (weight - weight_hi).astype(BF16)
    mix_part = dot(weight_hi.astype(BF16), out_rows, 0, 0) + dot(weight_lo, out_rows, 0, 0)
    mix_part = mix_part.astype(BF16)
    cross = dot(dout_col, out_rows, 1, 1) * pick.T.astype(F32)
    slot_expert = z_index * plane + jnp.arange(slots, dtype=jnp.int32) // per_expert
    dg_part = jnp.sum(
        jnp.where(
            routes_col[:, :, None] == slot_expert[None, None, :], cross[:, None, :], 0.0
        ),
        axis=2,
    )
    packed = jnp.concatenate([mix_part, padded(split3(dg_part), 128)], axis=1)

    def summed(parts, first, width):
        planes = [parts[i, :, first : first + width].astype(F32) for i in range(N_Z)]
        while len(planes) > 1:
            planes = [x + y for x, y in zip(planes[::2], planes[1::2])]
        return planes[0]

    mix_parts = to_column(packed)
    mixture = summed(mix_parts, 0, model_width).astype(BF16)
    dg_sum = summed(mix_parts, model_width, 3 * top_count)
    d_gates = (
        dg_sum[:, :top_count]
        + dg_sum[:, top_count : 2 * top_count]
        + dg_sum[:, 2 * top_count :]
    )
    back_rows = to_plane(d_rows)
    dtok_part = dot(pick, back_rows, 0, 0).astype(BF16)
    d_tokens = summed(to_column(dtok_part), 0, model_width).astype(BF16)
    return (mixture, d_tokens, d_gates, g_gate, g_up, g_down)


def solution(mesh):
    fine = Mesh(mesh.devices.reshape(-1, N_Z, N_X, N_CORE), ("dp", "z", "x", "core"))
    every = ("dp", "z", "x", "core")
    expert = ("z", "x", "core")
    return jax.shard_map(
        on_device,
        mesh=fine,
        in_specs=(
            P(every, None),
            P(every, None),
            P(every, None),
            P(expert, None, None),
            P(expert, None, None),
            P(expert, None, None),
            P(),
            P(every, None),
        ),
        out_specs=(
            P(every, None),
            P(every, None),
            P(every, None),
            P(expert, "dp", None),
            P(expert, "dp", None),
            P(expert, None, "dp"),
        ),
        check_vma=False,
    )
```

```python
import jax
import jax.numpy as jnp
from jax import lax
from jax.sharding import Mesh, PartitionSpec as P


N_Z, N_X, N_CORE = 8, 4, 2
PLANE = ("x", "core")
BF16, F32 = jnp.bfloat16, jnp.float32


def dot(left, right, lc=1, rc=0):
    return lax.dot_general(left, right, (((lc,), (rc,)), ((), ())), preferred_element_type=F32)


def split3(value):
    first = lax.reduce_precision(value, 8, 7)
    second = lax.reduce_precision(value - first, 8, 7)
    third = value - first - second
    return [part.astype(BF16) for part in (first, second, third)]


def padded(parts, width):
    used = sum(p.shape[1] for p in parts)
    return jnp.concatenate(parts + [jnp.zeros((parts[0].shape[0], width - used), BF16)], axis=1)


def on_device(tokens, routes, gates, w_gate, w_up, w_down, swap_flags, d_out):
    tok_count, model_width = tokens.shape
    top_count = routes.shape[1]
    plane = N_X * N_CORE
    experts = N_Z * plane
    capacity = min(tok_count, (3 * tok_count * top_count + 2 * experts - 1) // (2 * experts))
    column = N_Z * tok_count
    per_expert = N_Z * capacity
    slots = plane * per_expert
    z_index = lax.axis_index("z")
    own_index = (z_index * N_X + lax.axis_index("x")) * N_CORE + lax.axis_index("core")
    own_flag = swap_flags[own_index]
    gate_mat, up_mat, down_mat = w_gate[0], w_up[0], w_down[0]

    meta = padded([routes.astype(BF16)] + split3(gates), 128)
    gathered = lax.all_gather(jnp.concatenate([tokens, d_out, meta], axis=1), "z", tiled=True)
    tok_col = gathered[:, :model_width]
    dout_col = gathered[:, model_width : 2 * model_width]
    meta_col = gathered[:, 2 * model_width : 2 * model_width + 4 * top_count].astype(F32)
    routes_col = meta_col[:, :top_count].astype(jnp.int32)
    row = jnp.arange(column, dtype=jnp.int32)
    earlier = (
        (row[:, None] > row[None, :])
        & (row[:, None] // tok_count == row[None, :] // tok_count)
    ).astype(BF16)
    slot_ids = jnp.arange(slots, dtype=jnp.int32)
    spread = (
        slot_ids[:, None] // per_expert == jnp.arange(plane, dtype=jnp.int32)[None, :]
    ).astype(BF16)
    slot_rank = (slot_ids % per_expert).astype(F32)[:, None]
    first_rank = (row // tok_count * capacity).astype(F32)[:, None]

    def selection(ids, routes_col):
        named = routes_col[:, None, :] == ids[None, :, None]
        member = jnp.any(named, axis=2)
        rank = jnp.where(member, first_rank + dot(earlier, member.astype(BF16)), -1.0)
        return (dot(spread, rank.astype(BF16), 1, 1) == slot_rank).astype(BF16), named

    def to_plane(rows):
        rows = rows.reshape(plane, per_expert, -1)
        rows = lax.all_to_all(rows, PLANE, split_axis=0, concat_axis=0, tiled=True)
        return rows.reshape(slots, -1)

    def to_column(rows):
        rows = rows.reshape(N_Z, tok_count, -1)
        return lax.all_to_all(rows, "z", split_axis=0, concat_axis=0, tiled=True)

    def token_rows(pick):
        rows = dot(pick, tok_col).astype(BF16)
        return to_plane(rows)

    def cot_pairs(pick, slot_gate):
        rows = (slot_gate * dot(pick, dout_col)).astype(BF16)
        return to_plane(rows)

    plane_ids = z_index * plane + jnp.arange(plane, dtype=jnp.int32)
    pick, named = selection(plane_ids, routes_col)
    rows_in = token_rows(pick)
    gate_parts = [
        jnp.sum(
            jnp.where(named, meta_col[:, None, i * top_count : (i + 1) * top_count], 0.0), axis=2
        ).astype(BF16)
        for i in range(1, 4)
    ]
    slot_gate = jnp.sum(
        dot(pick, jnp.concatenate(gate_parts, axis=1)) * jnp.tile(spread, (1, 3)).astype(F32),
        axis=1,
        keepdims=True,
    )
    cot_rows = cot_pairs(pick, slot_gate)

    plane_flags = lax.dynamic_slice(swap_flags, (z_index * plane,), (plane,))
    later_routes, _ = lax.optimization_barrier((routes_col, rows_in))
    placed_pick, _ = selection(
        jnp.where(plane_flags == 1, plane_ids ^ (experts // 2), plane_ids), later_routes
    )
    placed_tok = token_rows(placed_pick)

    pre_gate = dot(rows_in, gate_mat)
    pre_up = dot(rows_in, up_mat)
    logistic = jax.nn.sigmoid(pre_gate)
    activated = pre_gate * logistic
    hidden = (activated * pre_up).astype(BF16)
    _, cot_rows = lax.optimization_barrier((hidden, cot_rows))
    d_hidden = dot(cot_rows, down_mat, 1, 1)
    grad_gate_pre = (d_hidden * pre_up * logistic * (1.0 + pre_gate * (1.0 - logistic))).astype(
        BF16
    )
    grad_up_pre = (d_hidden * activated).astype(BF16)
    result = dot(hidden, down_mat).astype(BF16)
    d_rows = (
        dot(grad_gate_pre, gate_mat, 1, 1) + dot(grad_up_pre, up_mat, 1, 1)
    ).astype(BF16)

    def placed(own):
        other = lax.ppermute(own, "z", [(i, i ^ (N_Z // 2)) for i in range(N_Z)])
        return jnp.where(own_flag == 1, other, own)

    def reduced(left, right):
        partial = dot(left, right, 0, 0).astype(BF16)
        return lax.psum_scatter(partial, "dp", scatter_dimension=0, tiled=True)

    g_down = placed(reduced(cot_rows, hidden)).T[None]
    g_gate = reduced(placed_tok, placed(grad_gate_pre))[None]
    g_up = reduced(placed_tok, placed(grad_up_pre))[None]

    out_rows = to_plane(result)
    weight = jnp.where(pick == 1, jnp.broadcast_to(slot_gate, pick.shape), 0.0)
    weight_hi = lax.reduce_precision(weight, 8, 7)
    weight_lo = (weight - weight_hi).astype(BF16)
    mix_part = dot(weight_hi.astype(BF16), out_rows, 0, 0) + dot(weight_lo, out_rows, 0, 0)
    mix_part = mix_part.astype(BF16)
    cross = dot(dout_col, out_rows, 1, 1) * pick.T.astype(F32)
    slot_expert = z_index * plane + jnp.arange(slots, dtype=jnp.int32) // per_expert
    dg_part = jnp.sum(
        jnp.where(routes_col[:, :, None] == slot_expert[None, None, :], cross[:, None, :], 0.0),
        axis=2,
    )
    back_rows = to_plane(d_rows)
    dtok_part = dot(pick, back_rows, 0, 0).astype(BF16)
    parts = to_column(jnp.concatenate([mix_part, dtok_part, padded(split3(dg_part), 128)], axis=1))

    def summed(first, width):
        planes = [parts[i, :, first : first + width].astype(F32) for i in range(N_Z)]
        while len(planes) > 1:
            planes = [x + y for x, y in zip(planes[::2], planes[1::2])]
        return planes[0]

    mixture = summed(0, model_width).astype(BF16)
    d_tokens = summed(model_width, model_width).astype(BF16)
    dg_sum = summed(2 * model_width, 3 * top_count)
    d_gates = (
        dg_sum[:, :top_count]
        + dg_sum[:, top_count : 2 * top_count]
        + dg_sum[:, 2 * top_count :]
    )
    return (mixture, d_tokens, d_gates, g_gate, g_up, g_down)


def solution(mesh):
    fine = Mesh(mesh.devices.reshape(-1, N_Z, N_X, N_CORE), ("dp", "z", "x", "core"))
    every = ("dp", "z", "x", "core")
    expert = ("z", "x", "core")
    return jax.shard_map(
        on_device,
        mesh=fine,
        in_specs=(
            P(every, None),
            P(every, None),
            P(every, None),
            P(expert, None, None),
            P(expert, None, None),
            P(expert, None, None),
            P(),
            P(every, None),
        ),
        out_specs=(
            P(every, None),
            P(every, None),
            P(every, None),
            P(expert, "dp", None),
            P(expert, "dp", None),
            P(expert, None, "dp"),
        ),
        check_vma=False,
    )
```
